768 devices in a mesh: occ: 6 (over z_lo, core), row: 8 (over y), col: 16 (over x, z_hi).
Axes of the slice: x: 4, y: 8, z: 12 (z_hi: 4, z_lo: 3; z = z_hi * 3 + z_lo), core: 2. Of those that a mesh axis runs over, the one named last changes fastest.
Arguments:
- bra_factor: bfloat16 [3072, 2, 4096], P(('occ', 'col'), None, 'row'), may hold values from -0.5 to 0.5
- ket_factor: bfloat16 [3072, 2, 4096], P(('occ', 'row'), None, 'col'), may hold values from -0.5 to 0.5
- occ_energy: float32 [2], replicated, may hold values from -2 to -0.5
- virt_energy: float32 [4096], replicated, may hold values from 0.2 to 3
Outputs:
- amplitudes: bfloat16 [2, 2, 4096, 4096], P(None, None, 'row', 'col')
- gamma: float32 [3072, 2, 4096], P(('occ', 'col'), None, 'row')
The draws below stay inside these ranges and needn't reach their ends.
All inputs are finite; a program needn't handle non-finite values.
Results may differ from the reference program's by a relative error of at most 0.002.
Values may be sent and summed in bfloat16 or wider, within the bound.
A program may use at most 32 MiB of HBM per device.

```python
import jax
import jax.numpy as jnp

NAUX = 3072
NVIRT = 4096
OCC_WIN = 2


def shard_levels(rng, shape, cuts, least, top_value):
    gain = 1.0
    for position, blocks in cuts:
        heights = jax.random.uniform(jax.random.fold_in(jax.random.fold_in(rng, 6), position), (blocks,), jnp.float32, least / len(cuts), top_value / len(cuts))
        gain = gain * jnp.repeat(jnp.exp(heights), shape[position] // blocks).reshape((-1,) + (1,) * (len(shape) - 1 - position))
    return gain


def centred(stream_key, shape, scale, reach, pieces=(), held_as=jnp.bfloat16):
    array = scale * jax.random.normal(stream_key, shape, jnp.float32)
    if pieces:
        array = array * shard_levels(stream_key, shape, pieces, -0.22, 0.18)
    return jnp.clip(array, -reach, reach).astype(held_as)


def setup_inputs(seed: int = 0) -> dict:
    key_list = jax.random.split(jax.random.key(seed), 5)
    return {
        "bra_factor": centred(key_list[0], (NAUX, OCC_WIN, NVIRT), 0.08, 0.5, ((0, 96), (2, 8))),
        "ket_factor": centred(key_list[1], (NAUX, OCC_WIN, NVIRT), 0.08, 0.5, ((0, 48), (2, 16))),
        "occ_energy": jnp.clip(jax.random.uniform(key_list[2], (OCC_WIN,), jnp.float32, -2.0, -0.5), -2.0, -0.5),
        "virt_energy": jnp.clip(jax.random.uniform(key_list[3], (NVIRT,), jnp.float32, 0.2, 3.0), 0.2, 3.0),
    }


def reference(bra_factor, ket_factor, occ_energy, virt_energy):
    bra_wide = bra_factor.astype(jnp.float32)
    ket_wide = ket_factor.astype(jnp.float32)
    coulomb = jnp.einsum("qia,qjb->ijab", bra_wide, ket_wide)
    denominator = (occ_energy[:, None, None, None] + occ_energy[None, :, None, None]
                   - virt_energy[None, None, :, None] - virt_energy[None, None, None, :])
    amplitudes = ((2.0 * coulomb - jnp.transpose(coulomb, (1, 0, 2, 3))) / denominator).astype(jnp.bfloat16)
    gamma = jnp.einsum("ijab,qjb->qia", amplitudes.astype(jnp.float32), ket_wide)
    return amplitudes, gamma
```

```python
import functools

import jax
import jax.numpy as jnp
from jax import lax
from jax.experimental import pallas as pl
from jax.experimental.pallas import tpu as pltpu
from jax.sharding import PartitionSpec as P

NZL, NC, NY, NX, NZH = 3, 2, 8, 4, 4
WIN = 192
STARTS = (0, 160, 320)
KEEP = 176
BF, F32 = jnp.bfloat16, jnp.float32
NT = (((1,), (1,)), ((), ()))
TN = (((0,), (0,)), ((), ()))


def rem(value, n):
    return lax.rem(value, n)


def kernel(
    occ_ref, bra_ref, ket_ref, virt_ref, amp_ref, gam_ref,
    bra_all, ket_all, part, other, amps, va_col,
    rx_send, rx_recv, rx_own, rz_send, rz_recv, rzb_send, rzb_recv,
    bz_s, bz_r, bx_s, bx_r, kz_s, kz_r, ky_s, ky_r, p_s, p_r,
    ag_s, ag_r, fw_s, fw_r, rx_s, rx_r, rz_s, rz_r,
):
    occ, y, col = lax.axis_index("occ"), lax.axis_index("row"), lax.axis_index("col")
    zl, core = occ // 2, rem(occ, 2)
    x, zh = col // 4, rem(col, 4)

    def device(dx=0, dy=0, dzh=0, dzl=0, dcore=0):
        zl2, core2 = rem(zl + dzl, NZL), rem(core + dcore, NC)
        y2, x2, zh2 = rem(y + dy, NY), rem(x + dx, NX), rem(zh + dzh, NZH)
        return (zl2 * 2 + core2, y2, x2 * 4 + zh2)

    def send(src, dst, s_sem, r_sem, **where):
        return pltpu.make_async_remote_copy(
            src_ref=src, dst_ref=dst, send_sem=s_sem, recv_sem=r_sem,
            device_id=device(**where), device_id_type=pl.DeviceIdType.MESH,
        )

    z_peers = [(e, d) for e in range(3) for d in range(4) if (e, d) != (0, 0)]
    peers = [dict(dzl=e, dzh=d) for e, d in z_peers]
    peers += [dict(dx=d) for d in (1, 2, 3)] + [dict(dy=1), dict(dy=NY - 1), dict(dcore=1)]
    barrier = pltpu.get_barrier_semaphore()
    for peer in peers:
        pl.semaphore_signal(barrier, inc=1, device_id=device(**peer), device_id_type=pl.DeviceIdType.MESH)
    pl.semaphore_wait(barrier, len(peers))

    pending = []

    def start(copy):
        copy.start()
        pending.append(copy)

    def bra_rows(zl_src, x_src, zh_src=0):
        return pl.multiple_of(zl_src * 512 + x_src * 128 + zh_src * 32, 32)

    def ket_rows(zl_src, y_src):
        return pl.multiple_of(zl_src * 512 + y_src * 64, 64)

    own_ket = ket_rows(zl, y)

    def ket_z(e):
        return send(ket_ref, ket_all.at[pl.ds(own_ket, 64)], kz_s.at[e], kz_r.at[e], dzl=e)

    def ket_y(e, way, step):
        zl_src = rem(zl + 3 - e, 3)
        hop = 1 if way == 0 else NY - 1
        y_src = rem(y + (NY - step + 1 if way == 0 else step - 1), NY)
        rows = ket_rows(zl_src, y_src)
        size = 64 if step < 4 else 32
        rows = pl.multiple_of(rows + (32 if step == 4 and way == 1 else 0), 32)
        here = ket_all.at[pl.ds(rows, size)]
        src = ket_ref if (step == 1 and e == 0) else here
        k = (e * 2 + way) * 4 + step - 1
        return send(src, here, ky_s.at[k], ky_r.at[k], dy=hop)

    def bra_z(e, d):
        there = bra_all.at[pl.ds(bra_rows(zl, x, zh), 32)]
        return send(bra_ref.at[rem(zl + e, 3)], there, bz_s.at[e * 4 + d], bz_r.at[e * 4 + d], dzl=e, dzh=d)

    def bra_x(e, dx):
        here = bra_all.at[pl.ds(bra_rows(rem(zl + 3 - e, 3), x), 128)]
        return send(here, here, bx_s.at[e * 3 + dx - 1], bx_r.at[e * 3 + dx - 1], dx=dx)

    for e in (1, 2):
        start(ket_z(e))
    for way in (0, 1):
        start(ket_y(0, way, 1))
    for e, d in [(0, 1), (0, 3), (0, 2)] + [(e, d) for e in (1, 2) for d in (0, 1, 3, 2)]:
        start(bra_z(e, d))
    ket_all[pl.ds(own_ket, 64), :] = ket_ref[...]
    bra_all[pl.ds(bra_rows(zl, x, zh), 32), :] = bra_ref[zl]

    for t in range(4):
        row = virt_ref[pl.ds(y * 4 + t, 1), :]
        va_col[pl.ds(t * 128, 128), :] = jnp.transpose(jnp.broadcast_to(row, (128, 128)))

    for e in (1, 2):
        ket_z(e).wait_recv()
        for way in (0, 1):
            start(ket_y(e, way, 1))

    for step in (2, 3, 4):
        e = step - 2
        for e2 in range(3):
            for way in (0, 1):
                ket_y(e2, way, step - 1).wait_recv()
                start(ket_y(e2, way, step))
        for d in range(4):
            if (e, d) != (0, 0):
                bra_z(e, d).wait_recv()
        for dx in (1, 2, 3):
            start(bra_x(e, dx))

    for e in range(3):
        for dx in (1, 2, 3):
            bra_x(e, dx).wait_recv()
        for way in (0, 1):
            ket_y(e, way, 4).wait_recv()
        rows = pl.ds(pl.multiple_of(rem(zl + 3 - e, 3) * 512, 512), 512)
        term = lax.dot_general(bra_all[rows, :], ket_all[rows, :], TN, preferred_element_type=F32)
        if e == 0:
            part[...] = term
        else:
            part[...] += term
    swap = send(part, other, p_s.at[0], p_r.at[0], dcore=1)
    start(swap)
    vb_rows = virt_ref[pl.ds(col * 2, 2), :]
    vb = jnp.concatenate([vb_rows[0:1], vb_rows[1:2]], axis=1)
    va = va_col[pl.ds(pl.multiple_of(zl * 160, 32), WIN), :]
    va = jnp.concatenate([va, va], axis=1)
    swap.wait_recv()

    def coulomb(i, j):
        rows, cols = pl.ds(i * WIN, WIN), pl.ds(j * 256, 256)
        return part[rows, cols] + other[rows, cols]

    for i in range(2):
        for j in range(2):
            den = ((occ_ref[i] + occ_ref[j]) - va) - vb
            amps[j, pl.ds(i * WIN, WIN), :] = ((2.0 * coulomb(i, j) - coulomb(j, i)) / den).astype(BF)
    skip = pl.multiple_of(jnp.where(zl == 2, WIN - KEEP, 0), 16)

    def amp_z(e):
        src = amps.at[:, pl.ds(pl.multiple_of(core * WIN + skip, 16), KEEP), :]
        return send(src, amp_ref.at[zl, core], ag_s.at[e], ag_r.at[e], dzl=e)

    def amp_core(e):
        here = amp_ref.at[rem(zl + 3 - e, 3), core]
        return send(here, here, fw_s.at[e], fw_r.at[e], dcore=1)

    def rx(e, dx):
        k = e * 3 + dx - 1
        return send(rx_send.at[k], rx_recv.at[k], rx_s.at[k], rx_r.at[k], dx=dx)

    def rz(e, d):
        k = e * 4 + d
        if d == 2:
            return send(rzb_send.at[e], rzb_recv.at[e], rz_s.at[k], rz_r.at[k], dzl=e, dzh=d)
        return send(rz_send.at[k], rz_recv.at[k], rz_s.at[k], rz_r.at[k], dzl=e, dzh=d)

    order = (1, 2, 0)
    for n, e in enumerate(order):
        for dx in (2, 1, 3, 0):
            rows = pl.ds(bra_rows(rem(zl + e, 3), rem(x + dx, 4)), 128)
            block = lax.dot_general(ket_all[rows, 0:256], amps[0], NT, preferred_element_type=F32)
            block += lax.dot_general(ket_all[rows, 256:512], amps[1], NT, preferred_element_type=F32)
            if dx == 0:
                rx_own[e] = block
            else:
                rx_send[e * 3 + dx - 1] = block.astype(BF)
                start(rx(e, dx))
        if n == 0:
            for e2 in (1, 2):
                start(amp_z(e2))
    for i in range(2):
        for j in range(2):
            amp_ref[zl, i, j] = amps[j, pl.ds(pl.multiple_of(i * WIN + skip, 16), KEEP), :]
    for e in order:
        for dx in (1, 2, 3):
            rx(e, dx).wait_recv()
        for d in (2, 1, 3, 0):
            rows = pl.ds(pl.multiple_of(rem(zh + d, 4) * 32, 32), 32)
            total = rx_own[e, rows, :]
            for dx in (1, 2, 3):
                total += rx_recv[e * 3 + dx - 1, rows, :].astype(F32)
            if d == 2:
                rzb_send[e] = total.astype(BF)
            else:
                rz_send[e * 4 + d] = total
            if (e, d) != (0, 0):
                start(rz(e, d))
    for e in (1, 2):
        amp_z(e).wait_recv()
        start(amp_core(e))
    for e in order:
        for d in range(4):
            if (e, d) != (0, 0):
                rz(e, d).wait_recv()
        first = rz_send[0] if e == 0 else rz_recv[e * 4]
        total = (first + rz_recv[e * 4 + 1]) + (rz_recv[e * 4 + 3] + rzb_recv[e].astype(F32))
        gam_ref[rem(zl + 3 - e, 3)] = total
    for e in (1, 2):
        amp_core(e).wait_recv()
    for copy in pending:
        copy.wait_send()


def on_device(bra_factor, ket_factor, occ_energy, virt_energy):
    windows = jnp.stack([bra_factor[:, :, s : s + WIN] for s in STARTS])
    dma = pltpu.SemaphoreType.DMA
    vmem = pl.BlockSpec(memory_space=pltpu.VMEM)
    amp, gam = pl.pallas_call(
        kernel,
        out_shape=(
            jax.ShapeDtypeStruct((3, 2, 2, KEEP, 256), BF),
            jax.ShapeDtypeStruct((3, 32, 2 * WIN), F32),
        ),
        in_specs=[pl.BlockSpec(memory_space=pltpu.SMEM), vmem, vmem, vmem],
        out_specs=(vmem, vmem),
        scratch_shapes=[
            pltpu.VMEM((1536, 2 * WIN), BF),
            pltpu.VMEM((1536, 512), BF),
            pltpu.VMEM((2 * WIN, 512), F32),
            pltpu.VMEM((2 * WIN, 512), F32),
            pltpu.VMEM((2, 2 * WIN, 256), BF),
            pltpu.VMEM((512, 128), F32),
            pltpu.VMEM((9, 128, 2 * WIN), BF),
            pltpu.VMEM((9, 128, 2 * WIN), BF),
            pltpu.VMEM((3, 128, 2 * WIN), F32),
            pltpu.VMEM((12, 32, 2 * WIN), F32),
            pltpu.VMEM((12, 32, 2 * WIN), F32),
            pltpu.VMEM((3, 32, 2 * WIN), BF),
            pltpu.VMEM((3, 32, 2 * WIN), BF),
            dma((12,)), dma((12,)), dma((9,)), dma((9,)), dma((3,)), dma((3,)),
            dma((24,)), dma((24,)), dma((1,)), dma((1,)),
            dma((3,)), dma((3,)), dma((3,)), dma((3,)), dma((9,)), dma((9,)), dma((12,)), dma((12,)),
        ],
        compiler_params=pltpu.CompilerParams(
            collective_id=0, has_side_effects=True, vmem_limit_bytes=48 << 20
        ),
    )(occ_energy, windows.reshape(3, 32, 2 * WIN), ket_factor.reshape(64, 512), virt_energy.reshape(32, 128))
    amplitudes = jnp.concatenate([amp[0], amp[1][:, :, 16:], amp[2]], axis=2)
    gam = gam.reshape(3, 32, 2, WIN)
    gamma = jnp.concatenate(
        [gam[0][:, :, :KEEP], gam[1][:, :, 16:KEEP], gam[2][:, :, 16:]], axis=2
    )
    return (amplitudes, gamma)


def solution(mesh):
    placed = (P(("occ", "col"), None, "row"), P(("occ", "row"), None, "col"), P(), P())
    return jax.shard_map(
        on_device,
        mesh=mesh,
        in_specs=placed,
        out_specs=(P(None, None, "row", "col"), P(("occ", "col"), None, "row")),
        check_vma=False,
    )
```

```python
import functools

import jax
import jax.numpy as jnp
from jax import lax
from jax.experimental import pallas as pl
from jax.experimental.pallas import tpu as pltpu
from jax.sharding import PartitionSpec as P

NZL, NC, NY, NX, NZH = 3, 2, 8, 4, 4
WIN = 192
STARTS = (0, 160, 320)
KEEP = 176
ROWS = ((0, 176, 0), (16, 160, 176), (16, 176, 336))
BF, F32 = jnp.bfloat16, jnp.float32
NT = (((1,), (1,)), ((), ()))
TN = (((0,), (0,)), ((), ()))


def rem(value, n):
    return lax.rem(value, n)


def kernel(
    occ_ref, bra_in, ket_in, virt_ref, amp_out, gam_out,
    occ_sm, virt_vm, bra_raw, ket_raw, bra_ref, ket_ref, amp_ref, gam_ref, bra_all, ket_all, part, other, amps, va_col,
    rx_send, rx_recv, rx_own, rz_own, rz_send, rz_recv, windows,
    in_sem, own_sem, got_sem, gam_sem, bz_s, bz_r, bx_s, bx_r, kz_s, kz_r, ky_s, ky_r, p_s, p_r,
    ag_s, ag_r, fw_s, fw_r, rx_s, rx_r, rz_s, rz_r,
):
    occ, y, col = lax.axis_index("occ"), lax.axis_index("row"), lax.axis_index("col")
    zl, core = occ // 2, rem(occ, 2)
    x, zh = col // 4, rem(col, 4)

    def device(dx=0, dy=0, dzh=0, dzl=0, dcore=0):
        zl2, core2 = rem(zl + dzl, NZL), rem(core + dcore, NC)
        y2, x2, zh2 = rem(y + dy, NY), rem(x + dx, NX), rem(zh + dzh, NZH)
        return (zl2 * 2 + core2, y2, x2 * 4 + zh2)

    def send(src, dst, s_sem, r_sem, **where):
        return pltpu.make_async_remote_copy(
            src_ref=src, dst_ref=dst, send_sem=s_sem, recv_sem=r_sem,
            device_id=device(**where), device_id_type=pl.DeviceIdType.MESH,
        )

    def bra_rows(zl_src, x_src, zh_src=0):
        return pl.multiple_of(zl_src * 512 + x_src * 128 + zh_src * 32, 32)

    def ket_rows(zl_src, y_src):
        return pl.multiple_of(zl_src * 512 + y_src * 64, 64)

    z_peers = [(e, d) for e in range(3) for d in range(4) if (e, d) != (0, 0)]
    peers = [dict(dzl=e, dzh=d) for e, d in z_peers]
    peers += [dict(dx=d) for d in (1, 2, 3)] + [dict(dy=1), dict(dy=NY - 1), dict(dcore=1)]
    barrier = pltpu.get_barrier_semaphore()
    for peer in peers:
        pl.semaphore_signal(barrier, inc=1, device_id=device(**peer), device_id_type=pl.DeviceIdType.MESH)
    loads = [
        pltpu.make_async_copy(src, dst, in_sem.at[k])
        for k, (src, dst) in enumerate(
            [(bra_in, bra_raw), (ket_in, ket_raw), (virt_ref, virt_vm), (occ_ref, occ_sm)]
        )
    ]
    for load in loads:
        load.start()
    own_ket = ket_rows(zl, y)
    loads[1].wait()
    ket_wide = ket_raw[...].astype(F32)
    ket_ref[...] = jnp.concatenate([ket_wide[:, 0, :], ket_wide[:, 1, :]], axis=1).astype(BF)
    ket_all[pl.ds(own_ket, 64), :] = ket_ref[...]
    loads[0].wait()
    bra_wide = bra_raw[...].astype(F32)
    lane = lax.broadcasted_iota(jnp.int32, (32, 2 * WIN), 1)
    for w in range(3):
        part0 = pltpu.roll(bra_wide[:, 0, :], (512 - STARTS[w]) % 512, 1)[:, : 2 * WIN]
        part1 = pltpu.roll(bra_wide[:, 1, :], (512 + WIN - STARTS[w]) % 512, 1)[:, : 2 * WIN]
        bra_ref[w] = jnp.where(lane < WIN, part0, part1).astype(BF)
    bra_all[pl.ds(bra_rows(zl, x, zh), 32), :] = bra_ref[zl]
    pl.semaphore_wait(barrier, len(peers))

    pending = []

    def start(copy):
        copy.start()
        pending.append(copy)

    def ket_z(e):
        return send(ket_ref, ket_all.at[pl.ds(own_ket, 64)], kz_s.at[e], kz_r.at[e], dzl=e)

    def ket_y(e, way, step):
        zl_src = rem(zl + 3 - e, 3)
        hop = 1 if way == 0 else NY - 1
        y_src = rem(y + (NY - step + 1 if way == 0 else step - 1), NY)
        rows = ket_rows(zl_src, y_src)
        size = 64 if step < 4 else 32
        rows = pl.multiple_of(rows + (32 if step == 4 and way == 1 else 0), 32)
        here = ket_all.at[pl.ds(rows, size)]
        src = ket_ref if (step == 1 and e == 0) else here
        k = (e * 2 + way) * 4 + step - 1
        return send(src, here, ky_s.at[k], ky_r.at[k], dy=hop)

    def bra_z(e, d):
        there = bra_all.at[pl.ds(bra_rows(zl, x, zh), 32)]
        return send(bra_ref.at[rem(zl + e, 3)], there, bz_s.at[e * 4 + d], bz_r.at[e * 4 + d], dzl=e, dzh=d)

    def bra_x(e, d, dx):
        here = bra_all.at[pl.ds(bra_rows(rem(zl + 3 - e, 3), x, rem(zh + 4 - d, 4)), 32)]
        k = (e * 4 + d) * 3 + dx - 1
        src = bra_ref.at[zl] if (e, d) == (0, 0) else here
        return send(src, here, bx_s.at[k], bx_r.at[k], dx=dx)

    def ket_on(e, step):
        for way in (0, 1):
            ket_y(e, way, step).wait_recv()
            start(ket_y(e, way, step + 1))

    def bra_on(e, d):
        bra_z(e, d).wait_recv()
        for dx in (2, 1, 3):
            start(bra_x(e, d, dx))

    for e in (1, 2):
        start(ket_z(e))
    for way in (0, 1):
        start(ket_y(0, way, 1))
    for dx in (2, 1, 3):
        start(bra_x(0, 0, dx))
    near = sorted(z_peers, key=lambda p: min((p[0] + 3 * p[1]) % 12, -(p[0] + 3 * p[1]) % 12))
    for e, d in near[:7]:
        start(bra_z(e, d))

    loads[2].wait()
    loads[3].wait()
    for t in range(4):
        row = virt_vm[pl.ds(y * 4 + t, 1), :]
        va_col[pl.ds(t * 128, 128), :] = jnp.transpose(jnp.broadcast_to(row, (128, 128)))

    ket_on(0, 1)
    for e in (1, 2):
        ket_z(e).wait_recv()
        for way in (0, 1):
            start(ket_y(e, way, 1))
    steps = [(0, 2), (1, 1), (2, 1), (0, 3), (1, 2), (2, 2), (1, 3), (2, 3)]
    for k in range(3):
        ket_on(*steps[k])
    for n, piece in enumerate(near):
        bra_on(*piece)
        if n + 7 < len(near):
            start(bra_z(*near[n + 7]))
        if n % 2 == 1:
            ket_on(*steps[3 + n // 2])

    for n, e in enumerate((1, 0, 2)):
        for d in range(4):
            for dx in (1, 2, 3):
                bra_x(e, d, dx).wait_recv()
        for way in (0, 1):
            ket_y(e, way, 4).wait_recv()
        rows = pl.ds(pl.multiple_of(rem(zl + 3 - e, 3) * 512, 512), 512)
        term = lax.dot_general(bra_all[rows, :], ket_all[rows, :], TN, preferred_element_type=F32)
        if n == 0:
            part[...] = term
        else:
            part[...] += term
    swap = send(part, other, p_s.at[0], p_r.at[0], dcore=1)
    start(swap)
    vb_rows = virt_vm[pl.ds(col * 2, 2), :]
    vb = jnp.concatenate([vb_rows[0:1], vb_rows[1:2]], axis=1)
    va = va_col[pl.ds(pl.multiple_of(zl * 160, 32), WIN), :]
    va = jnp.concatenate([va, va], axis=1)
    swap.wait_recv()

    def coulomb(i, j):
        rows, cols = pl.ds(i * WIN, WIN), pl.ds(j * 256, 256)
        return part[rows, cols] + other[rows, cols]

    for i in range(2):
        for j in range(2):
            den = ((occ_sm[i] + occ_sm[j]) - va) - vb
            amps[j, pl.ds(i * WIN, WIN), :] = ((2.0 * coulomb(i, j) - coulomb(j, i)) / den).astype(BF)
    skip = pl.multiple_of(jnp.where(zl == 2, WIN - KEEP, 0), 16)

    def amp_z(e):
        src = amps.at[:, pl.ds(pl.multiple_of(core * WIN + skip, 16), KEEP), :]
        return send(src, amp_ref.at[zl, core], ag_s.at[e], ag_r.at[e], dzl=e)

    def amp_core(e):
        here = amp_ref.at[rem(zl + 3 - e, 3), core]
        return send(here, here, fw_s.at[e], fw_r.at[e], dcore=1)

    def rx(e, dx):
        k = e * 3 + dx - 1
        return send(rx_send.at[k], rx_recv.at[k], rx_s.at[k], rx_r.at[k], dx=dx)

    def rz(e, d):
        k = e * 4 + d
        return send(rz_send.at[k], rz_recv.at[k], rz_s.at[k], rz_r.at[k], dzl=e, dzh=d)

    order = (1, 2, 0)
    for n, e in enumerate(order):
        for dx in (2, 1, 3, 0):
            rows = pl.ds(bra_rows(rem(zl + e, 3), rem(x + dx, 4)), 128)
            block = lax.dot_general(ket_all[rows, 0:256], amps[0], NT, preferred_element_type=F32)
            block += lax.dot_general(ket_all[rows, 256:512], amps[1], NT, preferred_element_type=F32)
            if dx == 0:
                rx_own[e] = block
            else:
                rx_send[e * 3 + dx - 1] = block.astype(BF)
                start(rx(e, dx))
        if n == 0:
            for e2 in (1, 2):
                start(amp_z(e2))
    def own_out(w, i):
        low, size, a0 = ROWS[w]
        src = amps.at[:, pl.ds(i * WIN + low, size), :]
        return pltpu.make_async_copy(src, amp_out.at[i, :, pl.ds(a0, size), :], own_sem.at[i])

    def got_out(w, e, half):
        low, size, a0 = ROWS[w]
        i = core if half == 0 else 1 - core
        src = amp_ref.at[w, i, :, pl.ds(low if w == 1 else 0, size), :]
        return pltpu.make_async_copy(src, amp_out.at[i, :, pl.ds(a0, size), :], got_sem.at[e * 2 + half])

    def by_window(which, act):
        for w in range(3):
            pl.when(which == w)(functools.partial(act, w))

    def own_start(w):
        for i in range(2):
            own_out(w, i).start()

    def own_wait(w):
        for i in range(2):
            own_out(w, i).wait()

    by_window(zl, own_start)
    for e in order:
        for dx in (1, 2, 3):
            rx(e, dx).wait_recv()
        for d in (2, 1, 3, 0):
            rows = pl.ds(pl.multiple_of(rem(zh + d, 4) * 32, 32), 32)
            total = rx_own[e, rows, :]
            for dx in (1, 2, 3):
                total += rx_recv[e * 3 + dx - 1, rows, :].astype(F32)
            if (e, d) == (0, 0):
                rz_own[...] = total
            else:
                rz_send[e * 4 + d] = total.astype(BF)
                start(rz(e, d))
    for e in (1, 2):
        amp_z(e).wait_recv()
        start(amp_core(e))
        by_window(rem(zl + 3 - e, 3), lambda w, e=e: got_out(w, e, 0).start())
    for e in order:
        for d in range(4):
            if (e, d) != (0, 0):
                rz(e, d).wait_recv()
        total = rz_own[...] if e == 0 else rz_recv[e * 4].astype(F32)
        for d in (1, 2, 3):
            total += rz_recv[e * 4 + d].astype(F32)
        windows[rem(zl + 3 - e, 3)] = total
    for e in (1, 2):
        amp_core(e).wait_recv()
        by_window(rem(zl + 3 - e, 3), lambda w, e=e: got_out(w, e, 1).start())
    lane = lax.broadcasted_iota(jnp.int32, (32, 512), 1)
    blank = jnp.zeros((32, 128), F32)
    wide = [jnp.concatenate([windows[w], blank], axis=1) for w in range(3)]
    for i in range(2):
        turn = [pltpu.roll(wide[w], (STARTS[w] - i * WIN) % 512, 1) for w in range(3)]
        gam_ref[:, i, :] = jnp.where(lane < 176, turn[0], jnp.where(lane < 336, turn[1], turn[2]))
    gamma_copy = pltpu.make_async_copy(gam_ref, gam_out, gam_sem)
    gamma_copy.start()
    by_window(zl, own_wait)
    for e in (1, 2):
        for half in range(2):
            by_window(rem(zl + 3 - e, 3), lambda w, e=e, half=half: got_out(w, e, half).wait())
    for copy in pending:
        copy.wait_send()
    gamma_copy.wait()


def on_device(bra_factor, ket_factor, occ_energy, virt_energy):
    dma = pltpu.SemaphoreType.DMA
    hbm = pl.BlockSpec(memory_space=pl.ANY)
    return pl.pallas_call(
        kernel,
        out_shape=(
            jax.ShapeDtypeStruct((2, 2, 512, 256), BF),
            jax.ShapeDtypeStruct((32, 2, 512), F32),
        ),
        in_specs=[hbm] * 4,
        out_specs=(hbm, hbm),
        scratch_shapes=[
            pltpu.SMEM((2,), F32),
            pltpu.VMEM((32, 128), F32),
            pltpu.VMEM((32, 2, 512), BF),
            pltpu.VMEM((64, 2, 256), BF),
            pltpu.VMEM((3, 32, 2 * WIN), BF),
            pltpu.VMEM((64, 512), BF),
            pltpu.VMEM((3, 2, 2, KEEP, 256), BF),
            pltpu.VMEM((32, 2, 512), F32),
            pltpu.VMEM((1536, 2 * WIN), BF),
            pltpu.VMEM((1536, 512), BF),
            pltpu.VMEM((2 * WIN, 512), F32),
            pltpu.VMEM((2 * WIN, 512), F32),
            pltpu.VMEM((2, 2 * WIN, 256), BF),
            pltpu.VMEM((512, 128), F32),
            pltpu.VMEM((9, 128, 2 * WIN), BF),
            pltpu.VMEM((9, 128, 2 * WIN), BF),
            pltpu.VMEM((3, 128, 2 * WIN), F32),
            pltpu.VMEM((32, 2 * WIN), F32),
            pltpu.VMEM((12, 32, 2 * WIN), BF),
            pltpu.VMEM((12, 32, 2 * WIN), BF),
            pltpu.VMEM((3, 32, 2 * WIN), F32),
            dma((4,)), dma((2,)), dma((6,)), dma, dma((12,)), dma((12,)), dma((36,)), dma((36,)), dma((3,)), dma((3,)),
            dma((24,)), dma((24,)), dma((1,)), dma((1,)),
            dma((3,)), dma((3,)), dma((3,)), dma((3,)), dma((9,)), dma((9,)), dma((12,)), dma((12,)),
        ],
        compiler_params=pltpu.CompilerParams(collective_id=0, has_side_effects=True),
    )(occ_energy, bra_factor, ket_factor, virt_energy.reshape(32, 128))


def solution(mesh):
    placed = (P(("occ", "col"), None, "row"), P(("occ", "row"), None, "col"), P(), P())
    return jax.shard_map(
        on_device,
        mesh=mesh,
        in_specs=placed,
        out_specs=(P(None, None, "row", "col"), P(("occ", "col"), None, "row")),
        check_vma=False,
    )
```

```python
import functools

import jax
import jax.numpy as jnp
from jax import lax
from jax.experimental import pallas as pl
from jax.experimental.pallas import tpu as pltpu
from jax.sharding import PartitionSpec as P

NZL, NC, NY, NX, NZH = 3, 2, 8, 4, 4
WIN = 192
STARTS = (0, 160, 320)
KEEP = 176
ROWS = ((0, 176, 0), (16, 160, 176), (16, 176, 336))
BF, F32 = jnp.bfloat16, jnp.float32
NT = (((1,), (1,)), ((), ()))
TN = (((0,), (0,)), ((), ()))


def rem(value, n):
    return lax.rem(value, n)


def kernel(
    occ_ref, bra_in, ket_in, virt_ref, amp_out, gam_out,
    occ_sm, virt_vm, bra_raw, ket_raw, bra_ref, ket_ref, amp_ref, gam_ref, bra_all, ket_all, part, other, amps, va_col,
    rx_send, rx_recv, rx_own, rz_own, rz_send, rz_recv, windows,
    in_sem, own_sem, got_sem, gam_sem, bz_s, bz_r, bx_s, bx_r, kz_s, kz_r, ky_s, ky_r, p_s, p_r,
    ag_s, ag_r, fw_s, fw_r, rx_s, rx_r, rz_s, rz_r,
):
    occ, y, col = lax.axis_index("occ"), lax.axis_index("row"), lax.axis_index("col")
    zl, core = occ // 2, rem(occ, 2)
    x, zh = col // 4, rem(col, 4)

    def device(dx=0, dy=0, dzh=0, dzl=0, dcore=0):
        zl2, core2 = rem(zl + dzl, NZL), rem(core + dcore, NC)
        y2, x2, zh2 = rem(y + dy, NY), rem(x + dx, NX), rem(zh + dzh, NZH)
        return (zl2 * 2 + core2, y2, x2 * 4 + zh2)

    def send(src, dst, s_sem, r_sem, **where):
        return pltpu.make_async_remote_copy(
            src_ref=src, dst_ref=dst, send_sem=s_sem, recv_sem=r_sem,
            device_id=device(**where), device_id_type=pl.DeviceIdType.MESH,
        )

    def bra_rows(zl_src, x_src, zh_src=0):
        return pl.multiple_of(zl_src * 512 + x_src * 128 + zh_src * 32, 32)

    def ket_rows(zl_src, y_src):
        return pl.multiple_of(zl_src * 512 + y_src * 64, 64)

    z_peers = [(e, d) for e in range(3) for d in range(4) if (e, d) != (0, 0)]
    peers = [dict(dzl=e, dzh=d) for e, d in z_peers]
    peers += [dict(dx=d) for d in (1, 2, 3)] + [dict(dy=1), dict(dy=NY - 1), dict(dcore=1)]
    loads = [
        pltpu.make_async_copy(src, dst, in_sem.at[k])
        for k, (src, dst) in enumerate(
            [(bra_in, bra_raw), (ket_in, ket_raw), (virt_ref, virt_vm), (occ_ref, occ_sm)]
        )
    ]
    for load in loads:
        load.start()
    barrier = pltpu.get_barrier_semaphore()
    for peer in peers:
        pl.semaphore_signal(barrier, inc=1, device_id=device(**peer), device_id_type=pl.DeviceIdType.MESH)
    own_ket = ket_rows(zl, y)
    loads[1].wait()
    ket_wide = ket_raw[...].astype(F32)
    ket_ref[...] = jnp.concatenate([ket_wide[:, 0, :], ket_wide[:, 1, :]], axis=1).astype(BF)
    ket_all[pl.ds(own_ket, 64), :] = ket_ref[...]
    pl.semaphore_wait(barrier, len(peers))

    pending = []

    def start(copy):
        copy.start()
        pending.append(copy)

    def ket_z(e):
        return send(ket_ref, ket_all.at[pl.ds(own_ket, 64)], kz_s.at[e], kz_r.at[e], dzl=e)

    def ket_y(e, way, step):
        zl_src = rem(zl + 3 - e, 3)
        hop = 1 if way == 0 else NY - 1
        y_src = rem(y + (NY - step + 1 if way == 0 else step - 1), NY)
        rows = ket_rows(zl_src, y_src)
        size = 64 if step < 4 else 32
        rows = pl.multiple_of(rows + (32 if step == 4 and way == 1 else 0), 32)
        here = ket_all.at[pl.ds(rows, size)]
        src = ket_ref if (step == 1 and e == 0) else here
        k = (e * 2 + way) * 4 + step - 1
        return send(src, here, ky_s.at[k], ky_r.at[k], dy=hop)

    def bra_z(e, d):
        there = bra_all.at[pl.ds(bra_rows(zl, x, zh), 32)]
        return send(bra_ref.at[rem(zl + e, 3)], there, bz_s.at[e * 4 + d], bz_r.at[e * 4 + d], dzl=e, dzh=d)

    def bra_x(e, d, dx):
        here = bra_all.at[pl.ds(bra_rows(rem(zl + 3 - e, 3), x, rem(zh + 4 - d, 4)), 32)]
        k = (e * 4 + d) * 3 + dx - 1
        src = bra_ref.at[zl] if (e, d) == (0, 0) else here
        return send(src, here, bx_s.at[k], bx_r.at[k], dx=dx)

    def ket_on(e, step):
        for way in (0, 1):
            ket_y(e, way, step).wait_recv()
            start(ket_y(e, way, step + 1))

    def bra_on(e, d):
        bra_z(e, d).wait_recv()
        for dx in (2, 1, 3):
            start(bra_x(e, d, dx))

    for e in (1, 2):
        start(ket_z(e))
    for way in (0, 1):
        start(ket_y(0, way, 1))
    near = sorted(z_peers, key=lambda p: min((p[0] + 3 * p[1]) % 12, -(p[0] + 3 * p[1]) % 12))
    loads[0].wait()
    bra_wide = bra_raw[...].astype(F32)
    lane = lax.broadcasted_iota(jnp.int32, (32, 2 * WIN), 1)
    for w in range(3):
        part0 = pltpu.roll(bra_wide[:, 0, :], (512 - STARTS[w]) % 512, 1)[:, : 2 * WIN]
        part1 = pltpu.roll(bra_wide[:, 1, :], (512 + WIN - STARTS[w]) % 512, 1)[:, : 2 * WIN]
        bra_ref[w] = jnp.where(lane < WIN, part0, part1).astype(BF)
    bra_all[pl.ds(bra_rows(zl, x, zh), 32), :] = bra_ref[zl]
    for e, d in near[:7]:
        start(bra_z(e, d))
    for dx in (2, 1, 3):
        start(bra_x(0, 0, dx))

    ket_on(0, 1)
    for e in (1, 2):
        ket_z(e).wait_recv()
        for way in (0, 1):
            start(ket_y(e, way, 1))
    steps = [(0, 2), (1, 1), (2, 1), (0, 3), (1, 2), (2, 2), (1, 3), (2, 3)]
    for k in range(3):
        ket_on(*steps[k])
    for n, piece in enumerate(near):
        bra_on(*piece)
        if n + 7 < len(near):
            start(bra_z(*near[n + 7]))
        if n % 2 == 1:
            ket_on(*steps[3 + n // 2])

    loads[2].wait()
    loads[3].wait()
    for t in range(4):
        row = virt_vm[pl.ds(y * 4 + t, 1), :]
        va_col[pl.ds(t * 128, 128), :] = jnp.transpose(jnp.broadcast_to(row, (128, 128)))

    for n, e in enumerate((1, 0, 2)):
        for d in range(4):
            for dx in (1, 2, 3):
                bra_x(e, d, dx).wait_recv()
        for way in (0, 1):
            ket_y(e, way, 4).wait_recv()
        rows = pl.ds(pl.multiple_of(rem(zl + 3 - e, 3) * 512, 512), 512)
        term = lax.dot_general(bra_all[rows, :], ket_all[rows, :], TN, preferred_element_type=F32)
        if n == 0:
            part[...] = term
        else:
            part[...] += term
    swap = send(part, other, p_s.at[0], p_r.at[0], dcore=1)
    start(swap)
    vb_rows = virt_vm[pl.ds(col * 2, 2), :]
    vb = jnp.concatenate([vb_rows[0:1], vb_rows[1:2]], axis=1)
    va = va_col[pl.ds(pl.multiple_of(zl * 160, 32), WIN), :]
    va = jnp.concatenate([va, va], axis=1)
    swap.wait_recv()

    def coulomb(i, j):
        rows, cols = pl.ds(i * WIN, WIN), pl.ds(j * 256, 256)
        return part[rows, cols] + other[rows, cols]

    for i in range(2):
        for j in range(2):
            den = ((occ_sm[i] + occ_sm[j]) - va) - vb
            amps[j, pl.ds(i * WIN, WIN), :] = ((2.0 * coulomb(i, j) - coulomb(j, i)) / den).astype(BF)
    skip = pl.multiple_of(jnp.where(zl == 2, WIN - KEEP, 0), 16)

    def amp_z(e):
        src = amps.at[:, pl.ds(pl.multiple_of(core * WIN + skip, 16), KEEP), :]
        return send(src, amp_ref.at[zl, core], ag_s.at[e], ag_r.at[e], dzl=e)

    def amp_core(e):
        here = amp_ref.at[rem(zl + 3 - e, 3), core]
        return send(here, here, fw_s.at[e], fw_r.at[e], dcore=1)

    def rx(e, dx):
        k = e * 3 + dx - 1
        return send(rx_send.at[k], rx_recv.at[k], rx_s.at[k], rx_r.at[k], dx=dx)

    def rz(e, d):
        k = e * 4 + d
        return send(rz_send.at[k], rz_recv.at[k], rz_s.at[k], rz_r.at[k], dzl=e, dzh=d)

    order = (1, 2, 0)
    for n, e in enumerate(order):
        for dx in (2, 1, 3, 0):
            rows = pl.ds(bra_rows(rem(zl + e, 3), rem(x + dx, 4)), 128)
            block = lax.dot_general(ket_all[rows, 0:256], amps[0], NT, preferred_element_type=F32)
            block += lax.dot_general(ket_all[rows, 256:512], amps[1], NT, preferred_element_type=F32)
            if dx == 0:
                rx_own[e] = block
            else:
                rx_send[e * 3 + dx - 1] = block.astype(BF)
                start(rx(e, dx))
        if n == 0:
            for e2 in (1, 2):
                start(amp_z(e2))
    def own_out(w, i):
        low, size, a0 = ROWS[w]
        src = amps.at[:, pl.ds(i * WIN + low, size), :]
        return pltpu.make_async_copy(src, amp_out.at[i, :, pl.ds(a0, size), :], own_sem.at[i])

    def got_out(w, e, half):
        low, size, a0 = ROWS[w]
        i = core if half == 0 else 1 - core
        src = amp_ref.at[w, i, :, pl.ds(low if w == 1 else 0, size), :]
        return pltpu.make_async_copy(src, amp_out.at[i, :, pl.ds(a0, size), :], got_sem.at[e * 2 + half])

    def by_window(which, act):
        for w in range(3):
            pl.when(which == w)(functools.partial(act, w))

    def own_start(w):
        for i in range(2):
            own_out(w, i).start()

    def own_wait(w):
        for i in range(2):
            own_out(w, i).wait()

    by_window(zl, own_start)
    for e in order:
        for dx in (1, 2, 3):
            rx(e, dx).wait_recv()
        for d in (2, 1, 3, 0):
            rows = pl.ds(pl.multiple_of(rem(zh + d, 4) * 32, 32), 32)
            total = rx_own[e, rows, :]
            for dx in (1, 2, 3):
                total += rx_recv[e * 3 + dx - 1, rows, :].astype(F32)
            if (e, d) == (0, 0):
                rz_own[...] = total
            else:
                rz_send[e * 4 + d] = total.astype(BF)
                start(rz(e, d))
    for e in (1, 2):
        amp_z(e).wait_recv()
        start(amp_core(e))
        by_window(rem(zl + 3 - e, 3), lambda w, e=e: got_out(w, e, 0).start())
    for e in order:
        for d in range(4):
            if (e, d) != (0, 0):
                rz(e, d).wait_recv()
        total = rz_own[...] if e == 0 else rz_recv[e * 4].astype(F32)
        for d in (1, 2, 3):
            total += rz_recv[e * 4 + d].astype(F32)
        windows[rem(zl + 3 - e, 3)] = total
    for e in (1, 2):
        amp_core(e).wait_recv()
        by_window(rem(zl + 3 - e, 3), lambda w, e=e: got_out(w, e, 1).start())
    lane = lax.broadcasted_iota(jnp.int32, (32, 512), 1)
    blank = jnp.zeros((32, 128), F32)
    wide = [jnp.concatenate([windows[w], blank], axis=1) for w in range(3)]
    for i in range(2):
        turn = [pltpu.roll(wide[w], (STARTS[w] - i * WIN) % 512, 1) for w in range(3)]
        gam_ref[:, i, :] = jnp.where(lane < 176, turn[0], jnp.where(lane < 336, turn[1], turn[2]))
    gamma_copy = pltpu.make_async_copy(gam_ref, gam_out, gam_sem)
    gamma_copy.start()
    by_window(zl, own_wait)
    for e in (1, 2):
        for half in range(2):
            by_window(rem(zl + 3 - e, 3), lambda w, e=e, half=half: got_out(w, e, half).wait())
    for copy in pending:
        copy.wait_send()
    gamma_copy.wait()


def on_device(bra_factor, ket_factor, occ_energy, virt_energy):
    dma = pltpu.SemaphoreType.DMA
    hbm = pl.BlockSpec(memory_space=pl.ANY)
    return pl.pallas_call(
        kernel,
        out_shape=(
            jax.ShapeDtypeStruct((2, 2, 512, 256), BF),
            jax.ShapeDtypeStruct((32, 2, 512), F32),
        ),
        in_specs=[hbm] * 4,
        out_specs=(hbm, hbm),
        scratch_shapes=[
            pltpu.SMEM((2,), F32),
            pltpu.VMEM((32, 128), F32),
            pltpu.VMEM((32, 2, 512), BF),
            pltpu.VMEM((64, 2, 256), BF),
            pltpu.VMEM((3, 32, 2 * WIN), BF),
            pltpu.VMEM((64, 512), BF),
            pltpu.VMEM((3, 2, 2, KEEP, 256), BF),
            pltpu.VMEM((32, 2, 512), F32),
            pltpu.VMEM((1536, 2 * WIN), BF),
            pltpu.VMEM((1536, 512), BF),
            pltpu.VMEM((2 * WIN, 512), F32),
            pltpu.VMEM((2 * WIN, 512), F32),
            pltpu.VMEM((2, 2 * WIN, 256), BF),
            pltpu.VMEM((512, 128), F32),
            pltpu.VMEM((9, 128, 2 * WIN), BF),
            pltpu.VMEM((9, 128, 2 * WIN), BF),
            pltpu.VMEM((3, 128, 2 * WIN), F32),
            pltpu.VMEM((32, 2 * WIN), F32),
            pltpu.VMEM((12, 32, 2 * WIN), BF),
            pltpu.VMEM((12, 32, 2 * WIN), BF),
            pltpu.VMEM((3, 32, 2 * WIN), F32),
            dma((4,)), dma((2,)), dma((6,)), dma, dma((12,)), dma((12,)), dma((36,)), dma((36,)), dma((3,)), dma((3,)),
            dma((24,)), dma((24,)), dma((1,)), dma((1,)),
            dma((3,)), dma((3,)), dma((3,)), dma((3,)), dma((9,)), dma((9,)), dma((12,)), dma((12,)),
        ],
        compiler_params=pltpu.CompilerParams(collective_id=0, has_side_effects=True),
    )(occ_energy, bra_factor, ket_factor, virt_energy.reshape(32, 128))


def solution(mesh):
    placed = (P(("occ", "col"), None, "row"), P(("occ", "row"), None, "col"), P(), P())
    return jax.shard_map(
        on_device,
        mesh=mesh,
        in_specs=placed,
        out_specs=(P(None, None, "row", "col"), P(("occ", "col"), None, "row")),
        check_vma=False,
    )
```

```python
import functools

import jax
import jax.numpy as jnp
from jax import lax
from jax.experimental import pallas as pl
from jax.experimental.pallas import tpu as pltpu
from jax.sharding import PartitionSpec as P

NZL, NC, NY, NX, NZH = 3, 2, 8, 4, 4
WIN = 192
STARTS = (0, 160, 320)
KEEP = 176
ROWS = ((0, 176, 0), (16, 160, 176), (16, 176, 336))
BF, F32 = jnp.bfloat16, jnp.float32
NT = (((1,), (1,)), ((), ()))
TN = (((0,), (0,)), ((), ()))


def rem(value, n):
    return lax.rem(value, n)


def kernel(
    occ_ref, bra_in, ket_in, virt_ref, amp_out, gam_out,
    occ_sm, virt_vm, bra_raw, ket_raw, bra_ref, ket_ref, amp_ref, gam_ref, bra_all, ket_all, part, other, amps, va_col,
    rx_send, rx_recv, rx_own, rz_own, rz_send, rz_recv, windows,
    in_sem, own_sem, got_sem, gam_sem, bz_s, bz_r, bx_s, bx_r, kz_s, kz_r, ky_s, ky_r, p_s, p_r,
    ag_s, ag_r, fw_s, fw_r, rx_s, rx_r, rz_s, rz_r,
):
    occ, y, col = lax.axis_index("occ"), lax.axis_index("row"), lax.axis_index("col")
    zl, core = occ // 2, rem(occ, 2)
    x, zh = col // 4, rem(col, 4)

    def device(dx=0, dy=0, dzh=0, dzl=0, dcore=0):
        zl2, core2 = rem(zl + dzl, NZL), rem(core + dcore, NC)
        y2, x2, zh2 = rem(y + dy, NY), rem(x + dx, NX), rem(zh + dzh, NZH)
        return (zl2 * 2 + core2, y2, x2 * 4 + zh2)

    def send(src, dst, s_sem, r_sem, **where):
        return pltpu.make_async_remote_copy(
            src_ref=src, dst_ref=dst, send_sem=s_sem, recv_sem=r_sem,
            device_id=device(**where), device_id_type=pl.DeviceIdType.MESH,
        )

    def bra_rows(zl_src, x_src, zh_src=0):
        return pl.multiple_of(zl_src * 512 + x_src * 128 + zh_src * 32, 32)

    def ket_rows(zl_src, y_src):
        return pl.multiple_of(zl_src * 512 + y_src * 64, 64)

    z_peers = [(e, d) for e in range(3) for d in range(4) if (e, d) != (0, 0)]
    peers = [dict(dzl=e, dzh=d) for e, d in z_peers]
    peers += [dict(dx=d) for d in (1, 2, 3)] + [dict(dy=1), dict(dy=NY - 1), dict(dcore=1)]
    loads = [
        pltpu.make_async_copy(src, dst, in_sem.at[k])
        for k, (src, dst) in enumerate(
            [(bra_in, bra_raw), (ket_in, ket_raw), (virt_ref, virt_vm), (occ_ref, occ_sm)]
        )
    ]
    for load in loads:
        load.start()
    barrier = pltpu.get_barrier_semaphore()
    for peer in peers:
        pl.semaphore_signal(barrier, inc=1, device_id=device(**peer), device_id_type=pl.DeviceIdType.MESH)
    own_ket = ket_rows(zl, y)
    loads[1].wait()
    ket_wide = ket_raw[...].astype(F32)
    ket_ref[...] = jnp.concatenate([ket_wide[:, 0, :], ket_wide[:, 1, :]], axis=1).astype(BF)
    ket_all[pl.ds(own_ket, 64), :] = ket_ref[...]
    pl.semaphore_wait(barrier, len(peers))

    pending = []

    def start(copy):
        copy.start()
        pending.append(copy)

    def ket_z(e):
        return send(ket_ref, ket_all.at[pl.ds(own_ket, 64)], kz_s.at[e], kz_r.at[e], dzl=e)

    def ket_y(e, way, step):
        zl_src = rem(zl + 3 - e, 3)
        hop = 1 if way == 0 else NY - 1
        y_src = rem(y + (NY - step + 1 if way == 0 else step - 1), NY)
        rows = ket_rows(zl_src, y_src)
        size = 64 if step < 4 else 32
        rows = pl.multiple_of(rows + (32 if step == 4 and way == 1 else 0), 32)
        here = ket_all.at[pl.ds(rows, size)]
        src = ket_ref if (step == 1 and e == 0) else here
        k = (e * 2 + way) * 4 + step - 1
        return send(src, here, ky_s.at[k], ky_r.at[k], dy=hop)

    def bra_z(e, d):
        there = bra_all.at[pl.ds(bra_rows(zl, x, zh), 32)]
        return send(bra_ref.at[rem(zl + e, 3)], there, bz_s.at[e * 4 + d], bz_r.at[e * 4 + d], dzl=e, dzh=d)

    def bra_x(e, d, dx):
        here = bra_all.at[pl.ds(bra_rows(rem(zl + 3 - e, 3), x, rem(zh + 4 - d, 4)), 32)]
        k = (e * 4 + d) * 3 + dx - 1
        src = bra_ref.at[zl] if (e, d) == (0, 0) else here
        return send(src, here, bx_s.at[k], bx_r.at[k], dx=dx)

    def ket_on(e, step):
        for way in (0, 1):
            ket_y(e, way, step).wait_recv()
            start(ket_y(e, way, step + 1))

    def bra_on(e, d):
        bra_z(e, d).wait_recv()
        for dx in (1, 3, 2):
            start(bra_x(e, d, dx))

    for e in (1, 2):
        start(ket_z(e))
    for way in (0, 1):
        start(ket_y(0, way, 1))
    near = sorted(z_peers, key=lambda p: min((p[0] + 3 * p[1]) % 12, -(p[0] + 3 * p[1]) % 12))
    loads[0].wait()
    bra_wide = bra_raw[...].astype(F32)
    lane = lax.broadcasted_iota(jnp.int32, (32, 2 * WIN), 1)
    for w in range(3):
        part0 = pltpu.roll(bra_wide[:, 0, :], (512 - STARTS[w]) % 512, 1)[:, : 2 * WIN]
        part1 = pltpu.roll(bra_wide[:, 1, :], (512 + WIN - STARTS[w]) % 512, 1)[:, : 2 * WIN]
        bra_ref[w] = jnp.where(lane < WIN, part0, part1).astype(BF)
    bra_all[pl.ds(bra_rows(zl, x, zh), 32), :] = bra_ref[zl]
    for e, d in near[:7]:
        start(bra_z(e, d))
    for dx in (1, 3, 2):
        start(bra_x(0, 0, dx))

    ket_on(0, 1)
    for e in (1, 2):
        ket_z(e).wait_recv()
        for way in (0, 1):
            start(ket_y(e, way, 1))
    steps = [(0, 2), (1, 1), (2, 1), (0, 3), (1, 2), (2, 2), (1, 3), (2, 3)]
    for k in range(3):
        ket_on(*steps[k])
    for n, piece in enumerate(near):
        bra_on(*piece)
        if n + 7 < len(near):
            start(bra_z(*near[n + 7]))
        if n % 2 == 1:
            ket_on(*steps[3 + n // 2])

    loads[2].wait()
    loads[3].wait()
    for t in range(4):
        row = virt_vm[pl.ds(y * 4 + t, 1), :]
        va_col[pl.ds(t * 128, 128), :] = jnp.transpose(jnp.broadcast_to(row, (128, 128)))

    for n, e in enumerate((1, 0, 2)):
        for d in range(4):
            for dx in (1, 2, 3):
                bra_x(e, d, dx).wait_recv()
        for way in (0, 1):
            ket_y(e, way, 4).wait_recv()
        rows = pl.ds(pl.multiple_of(rem(zl + 3 - e, 3) * 512, 512), 512)
        term = lax.dot_general(bra_all[rows, :], ket_all[rows, :], TN, preferred_element_type=F32)
        if n == 0:
            part[...] = term
        else:
            part[...] += term
    swap = send(part, other, p_s.at[0], p_r.at[0], dcore=1)
    start(swap)
    vb_rows = virt_vm[pl.ds(col * 2, 2), :]
    vb = jnp.concatenate([vb_rows[0:1], vb_rows[1:2]], axis=1)
    va = va_col[pl.ds(pl.multiple_of(zl * 160, 32), WIN), :]
    va = jnp.concatenate([va, va], axis=1)
    swap.wait_recv()

    def coulomb(i, j):
        rows, cols = pl.ds(i * WIN, WIN), pl.ds(j * 256, 256)
        return part[rows, cols] + other[rows, cols]

    for i in range(2):
        for j in range(2):
            den = ((occ_sm[i] + occ_sm[j]) - va) - vb
            amps[j, pl.ds(i * WIN, WIN), :] = ((2.0 * coulomb(i, j) - coulomb(j, i)) / den).astype(BF)
    skip = pl.multiple_of(jnp.where(zl == 2, WIN - KEEP, 0), 16)

    def amp_z(e):
        src = amps.at[:, pl.ds(pl.multiple_of(core * WIN + skip, 16), KEEP), :]
        return send(src, amp_ref.at[zl, core], ag_s.at[e], ag_r.at[e], dzl=e)

    def amp_core(e):
        here = amp_ref.at[rem(zl + 3 - e, 3), core]
        return send(here, here, fw_s.at[e], fw_r.at[e], dcore=1)

    def rx(e, dx):
        k = e * 3 + dx - 1
        return send(rx_send.at[k], rx_recv.at[k], rx_s.at[k], rx_r.at[k], dx=dx)

    def rz(e, d):
        k = e * 4 + d
        return send(rz_send.at[k], rz_recv.at[k], rz_s.at[k], rz_r.at[k], dzl=e, dzh=d)

    order = (1, 2, 0)
    for n, e in enumerate(order):
        for dx in (2, 1, 3, 0):
            rows = pl.ds(bra_rows(rem(zl + e, 3), rem(x + dx, 4)), 128)
            block = lax.dot_general(ket_all[rows, 0:256], amps[0], NT, preferred_element_type=F32)
            block += lax.dot_general(ket_all[rows, 256:512], amps[1], NT, preferred_element_type=F32)
            if dx == 0:
                rx_own[e] = block
            else:
                rx_send[e * 3 + dx - 1] = block.astype(BF)
                start(rx(e, dx))
        if n == 0:
            for e2 in (1, 2):
                start(amp_z(e2))
    def own_out(w, i):
        low, size, a0 = ROWS[w]
        src = amps.at[:, pl.ds(i * WIN + low, size), :]
        return pltpu.make_async_copy(src, amp_out.at[i, :, pl.ds(a0, size), :], own_sem.at[i])

    def got_out(w, e, half):
        low, size, a0 = ROWS[w]
        i = core if half == 0 else 1 - core
        src = amp_ref.at[w, i, :, pl.ds(low if w == 1 else 0, size), :]
        return pltpu.make_async_copy(src, amp_out.at[i, :, pl.ds(a0, size), :], got_sem.at[e * 2 + half])

    def by_window(which, act):
        for w in range(3):
            pl.when(which == w)(functools.partial(act, w))

    def own_start(w):
        for i in range(2):
            own_out(w, i).start()

    def own_wait(w):
        for i in range(2):
            own_out(w, i).wait()

    by_window(zl, own_start)
    for e in order:
        for dx in (1, 2, 3):
            rx(e, dx).wait_recv()
        for d in (2, 1, 3, 0):
            rows = pl.ds(pl.multiple_of(rem(zh + d, 4) * 32, 32), 32)
            total = rx_own[e, rows, :]
            for dx in (1, 2, 3):
                total += rx_recv[e * 3 + dx - 1, rows, :].astype(F32)
            if (e, d) == (0, 0):
                rz_own[...] = total
            else:
                rz_send[e * 4 + d] = total.astype(BF)
                start(rz(e, d))
    for e in (1, 2):
        amp_z(e).wait_recv()
        start(amp_core(e))
        by_window(rem(zl + 3 - e, 3), lambda w, e=e: got_out(w, e, 0).start())
    for e in order:
        for d in range(4):
            if (e, d) != (0, 0):
                rz(e, d).wait_recv()
        total = rz_own[...] if e == 0 else rz_recv[e * 4].astype(F32)
        for d in (1, 2, 3):
            total += rz_recv[e * 4 + d].astype(F32)
        windows[rem(zl + 3 - e, 3)] = total
    for e in (1, 2):
        amp_core(e).wait_recv()
        by_window(rem(zl + 3 - e, 3), lambda w, e=e: got_out(w, e, 1).start())
    lane = lax.broadcasted_iota(jnp.int32, (32, 512), 1)
    blank = jnp.zeros((32, 128), F32)
    wide = [jnp.concatenate([windows[w], blank], axis=1) for w in range(3)]
    for i in range(2):
        turn = [pltpu.roll(wide[w], (STARTS[w] - i * WIN) % 512, 1) for w in range(3)]
        gam_ref[:, i, :] = jnp.where(lane < 176, turn[0], jnp.where(lane < 336, turn[1], turn[2]))
    gamma_copy = pltpu.make_async_copy(gam_ref, gam_out, gam_sem)
    gamma_copy.start()
    by_window(zl, own_wait)
    for e in (1, 2):
        for half in range(2):
            by_window(rem(zl + 3 - e, 3), lambda w, e=e, half=half: got_out(w, e, half).wait())
    for copy in pending:
        copy.wait_send()
    gamma_copy.wait()


def on_device(bra_factor, ket_factor, occ_energy, virt_energy):
    dma = pltpu.SemaphoreType.DMA
    hbm = pl.BlockSpec(memory_space=pl.ANY)
    return pl.pallas_call(
        kernel,
        out_shape=(
            jax.ShapeDtypeStruct((2, 2, 512, 256), BF),
            jax.ShapeDtypeStruct((32, 2, 512), F32),
        ),
        in_specs=[hbm] * 4,
        out_specs=(hbm, hbm),
        scratch_shapes=[
            pltpu.SMEM((2,), F32),
            pltpu.VMEM((32, 128), F32),
            pltpu.VMEM((32, 2, 512), BF),
            pltpu.VMEM((64, 2, 256), BF),
            pltpu.VMEM((3, 32, 2 * WIN), BF),
            pltpu.VMEM((64, 512), BF),
            pltpu.VMEM((3, 2, 2, KEEP, 256), BF),
            pltpu.VMEM((32, 2, 512), F32),
            pltpu.VMEM((1536, 2 * WIN), BF),
            pltpu.VMEM((1536, 512), BF),
            pltpu.VMEM((2 * WIN, 512), F32),
            pltpu.VMEM((2 * WIN, 512), F32),
            pltpu.VMEM((2, 2 * WIN, 256), BF),
            pltpu.VMEM((512, 128), F32),
            pltpu.VMEM((9, 128, 2 * WIN), BF),
            pltpu.VMEM((9, 128, 2 * WIN), BF),
            pltpu.VMEM((3, 128, 2 * WIN), F32),
            pltpu.VMEM((32, 2 * WIN), F32),
            pltpu.VMEM((12, 32, 2 * WIN), BF),
            pltpu.VMEM((12, 32, 2 * WIN), BF),
            pltpu.VMEM((3, 32, 2 * WIN), F32),
            dma((4,)), dma((2,)), dma((6,)), dma, dma((12,)), dma((12,)), dma((36,)), dma((36,)), dma((3,)), dma((3,)),
            dma((24,)), dma((24,)), dma((1,)), dma((1,)),
            dma((3,)), dma((3,)), dma((3,)), dma((3,)), dma((9,)), dma((9,)), dma((12,)), dma((12,)),
        ],
        compiler_params=pltpu.CompilerParams(collective_id=0, has_side_effects=True),
    )(occ_energy, bra_factor, ket_factor, virt_energy.reshape(32, 128))


def solution(mesh):
    placed = (P(("occ", "col"), None, "row"), P(("occ", "row"), None, "col"), P(), P())
    return jax.shard_map(
        on_device,
        mesh=mesh,
        in_specs=placed,
        out_specs=(P(None, None, "row", "col"), P(("occ", "col"), None, "row")),
        check_vma=False,
    )
```
